32 devices in a mesh: pb: 8 (over z, y), ka: 2 (over x), ha: 2 (over core).
Axes of the slice: x: 2, y: 2, z: 4, core: 2. Of those that a mesh axis runs over, the one named last changes fastest.
Arguments:
- queries: bfloat16 [8192, 256], P(('pb', 'ka'), 'ha'), may hold values from -130 to 130
- key_codes: int32 [8192, 256], P(('ka', 'pb'), 'ha'), may hold values from -127 to 127
- value_codes: int32 [8192, 256], P(('ka', 'pb'), 'ha'), may hold values from -127 to 127
- key_scale: float32 [], replicated, may hold values from 0.015 to 0.02
- value_scale: float32 [], replicated, may hold values from 0.01 to 0.02
- out_grad: bfloat16 [8192, 256], P(('pb', 'ka'), 'ha'), may hold values from -256 to 256
Outputs:
- query_grad: float32 [8192, 256], P(('pb', 'ka'), 'ha')
- key_grad: float32 [8192, 256], P(('ka', 'pb'), 'ha')
- value_grad: float32 [8192, 256], P(('ka', 'pb'), 'ha')
The draws below stay inside these ranges and needn't reach their ends.
All inputs are finite; a program needn't handle non-finite values.
Results may differ from the reference program's by a relative error of at most 0.017.
Values may be sent and summed in bfloat16 or wider, within the bound.
A program may use at most 128 MiB of HBM per device.

```python
import math
import jax
import jax.numpy as jnp
import numpy as np
from jax import lax

HD = 128
HEADS = 2
SEQ = 8192


def shared_codes(key):
    base = jax.random.fold_in(key, 11)
    code_key, scale_key = jax.random.split(base)
    raw = jax.random.randint(code_key, (SEQ, HEADS * HD), -127, 128).astype(jnp.int32)
    positions = jnp.arange(SEQ, dtype=jnp.int32)
    limits = 107 + 20 * (positions + 1) // SEQ
    table = raw * limits[:, None] // 127
    table = jnp.clip(table, -127, 127).astype(jnp.int32)
    anchors = np.array([index * SEQ // 8 + SEQ // 16 for index in range(8)])
    lasts = np.array([head * HD + HD - 1 for head in range(HEADS)])
    table = table.at[anchors + 1].set(table[anchors])
    table = table.at[anchors[:, None], lasts[None, :]].set(127)
    table = table.at[anchors[:, None] + 1, lasts[None, :]].set(102)
    table = table.at[SEQ - 1, 0].set(-127)
    factor = jnp.exp(jax.random.uniform(scale_key, (), jnp.float32, math.log(0.015), math.log(0.02)))
    return (table, factor)


def draw_key_codes(key, part):
    return shared_codes(key)[0]


def draw_key_scale(key, part):
    return shared_codes(key)[1]


def draw_queries(key, part):
    result = 2.0 * jax.random.normal(jax.random.fold_in(key, 5), (SEQ, HEADS * HD), jnp.float32)
    return result.astype(jnp.bfloat16)


def set_ends(values, key, low, top_value):
    dims = values.shape
    place = [jax.random.randint(jax.random.fold_in(key, axis), (), 0, dims[axis]) for axis in range(len(dims))]
    values = values.at[tuple(place)].set(low)
    longest = dims.index(max(dims))
    place[longest] = (place[longest] + 1) % dims[longest]
    return values.at[tuple(place)].set(top_value)


def block_scale(own_key, extent, pieces, least, largest):
    def one(axis_at, shards_of):
        heights = jax.random.uniform(jax.random.fold_in(jax.random.fold_in(own_key, 6), axis_at), (shards_of,), jnp.float32, least / len(pieces), largest / len(pieces))
        return jnp.repeat(jnp.exp(heights), extent[axis_at] // shards_of).reshape((-1,) + (1,) * (len(extent) - axis_at - 1))

    gain = one(*pieces[0])
    for cut in pieces[1:]:
        gain = gain * one(*cut)
    return gain


def scatter_about(rng, shape, deviation, limit, cuts=(), held_as=jnp.bfloat16):
    values = jax.random.normal(rng, shape, jnp.float32) * deviation
    if len(cuts) > 0:
        values = block_scale(rng, shape, cuts, -0.22, 0.18) * values
    return jnp.clip(values, min=-limit, max=limit).astype(held_as)


def setup_inputs(seed: int = 0) -> dict:
    streams_of = jax.random.split(jax.random.key(seed), 7)
    queries = draw_queries(jax.random.fold_in(streams_of[6], 71), 0)
    key_codes = draw_key_codes(jax.random.fold_in(streams_of[6], 71), 0)
    value_codes = set_ends(jax.random.randint(streams_of[2], (SEQ, HEADS * HD), -127, 128), jax.random.fold_in(streams_of[2], 1), -127, 127).astype(jnp.int32)
    key_scale = draw_key_scale(jax.random.fold_in(streams_of[6], 71), 0)
    value_scale = jnp.clip(jnp.exp(jax.random.uniform(streams_of[4], (), jnp.float32, math.log(0.01), math.log(0.02))), 0.01, 0.02)
    out_grad = scatter_about(streams_of[5], (SEQ, HEADS * HD), (0.5 * SEQ ** 0.5), 256.0, ((0, 16), (1, 2)))
    return dict(queries=queries, key_codes=key_codes, value_codes=value_codes, key_scale=key_scale, value_scale=value_scale, out_grad=out_grad)


def dequantize(table, factor):
    return (table.astype(jnp.float32) * factor).astype(jnp.bfloat16)

def contract_last(left, right):
    return lax.dot_general(left, right, (((1,), (1,)), ((), ())), preferred_element_type=jnp.float32)

def contract_first(left, right):
    return lax.dot_general(left, right, (((0,), (0,)), ((), ())), preferred_element_type=jnp.float32)

def reference(queries, key_codes, value_codes, key_scale, value_scale, out_grad):
    keys = dequantize(key_codes, key_scale)
    values = dequantize(value_codes, value_scale)
    factor = 1.0 / math.sqrt(HD)
    block_rows = 1024 if SEQ % 1024 == 0 else SEQ
    block_count = SEQ // block_rows
    q_parts, k_parts, v_parts = ([], [], [])
    for head in range(HEADS):
        cols = slice(head * HD, (head + 1) * HD)
        q_head = queries[:, cols].reshape(block_count, block_rows, HD)
        d_head = out_grad[:, cols].reshape(block_count, block_rows, HD)
        k_head = keys[:, cols]
        v_head = values[:, cols]

        def step(totals, inputs):
            k_grad, v_grad = totals
            q_block, d_block = inputs
            scores = contract_last(q_block, k_head) * factor
            row_max = lax.optimization_barrier(jnp.max(scores, axis=1, keepdims=True))
            log_total = row_max + jnp.log(lax.optimization_barrier(jnp.sum(jnp.exp(scores - row_max), axis=1, keepdims=True)))
            probs = jnp.exp(scores - log_total)
            d_probs = contract_last(d_block, v_head)
            row_delta = lax.optimization_barrier(jnp.sum(probs * d_probs, axis=1, keepdims=True))
            d_scores = probs * (d_probs - row_delta)
            probs_low = probs.astype(jnp.bfloat16)
            d_scores_low = d_scores.astype(jnp.bfloat16)
            q_grad = jnp.dot(d_scores_low, k_head, preferred_element_type=jnp.float32) * factor
            k_grad = k_grad + contract_first(d_scores_low, q_block) * factor
            v_grad = v_grad + contract_first(probs_low, d_block)
            return ((k_grad, v_grad), q_grad)
        zeros = jnp.zeros((SEQ, HD), jnp.float32)
        (k_grad, v_grad), q_grad = lax.scan(step, (zeros, zeros), (q_head, d_head))
        q_parts.append(q_grad.reshape(SEQ, HD))
        k_parts.append(k_grad)
        v_parts.append(v_grad)
    return (jnp.concatenate(q_parts, axis=1), jnp.concatenate(k_parts, axis=1), jnp.concatenate(v_parts, axis=1))
```

```python
import functools
import math

import jax
import jax.numpy as jnp
from jax import lax
from jax.experimental import pallas as pl
from jax.experimental.pallas import tpu as pltpu
from jax.sharding import PartitionSpec as P

MESH = pl.DeviceIdType.MESH
LOW = jnp.bfloat16
CHUNKS = 4
WINDOW = 2
UNROLL = 8
WIDE = jnp.float32


def flipped(rank, step, count):
    total = 0
    bit = 1
    while bit < count:
        one = (rank // bit) % 2
        two = (step // bit) % 2
        total = total + bit * (one + two - 2 * one * two)
        bit *= 2
    return total


def contract(left, right, dims):
    return lax.dot_general(left, right, ((dims[:1], dims[1:]), ((), ())), preferred_element_type=WIDE)


def order(index, near, far, evens, subs):
    late = jnp.maximum(index - near * subs, 0) if not isinstance(index, int) else max(index - near * subs, 0)
    is_late = (index >= near * subs) * 1
    spot = late % max(far, 1)
    if evens:
        spot = 2 * (spot % evens) + spot // evens
    step = is_late * (near + spot) + (1 - is_late) * (index // subs)
    part = is_late * (late // max(far, 1)) + (1 - is_late) * (index % subs)
    return step, part


def kernel(
    nq, nk, nka, subs,
    key_scale, value_scale, q_ref, g_ref, kc_ref, vc_ref,
    dq_ref, dk_ref, dv_ref,
    qd, kv, codes, held_e, held_d, shift, top, total, dot, stats, lse, delta, acc_q, acc_k, acc_v,
    gk_out, gk_mid, gk_in, gq_out, gq_mid, gq_in,
    load, q_send, q_recv, k_send, k_recv, s_send, s_recv,
    gk_send, gk_mid_recv, gk_recv, gq_send, gq_mid_recv, gq_recv,
):
    rows, width = q_ref.shape
    piece, slab = rows // CHUNKS, rows // subs
    factor = 1.0 / math.sqrt(width)
    log2e = math.log2(math.e)
    pb, ka = lax.axis_index("pb"), lax.axis_index("ka")
    my_a, my_k = pb // nk, pb % nk
    my_q = my_a * nka + ka
    near_u, near_w, far_w, even_w = nka * subs, 2 * subs, nk - 2, nk // 2 - 1

    def q_rank(step):
        return flipped(my_q, step, nq)

    def q_peer(step):
        rank = q_rank(step)
        return {"pb": (rank // nka) * nk + my_k, "ka": rank % nka}

    def k_peer(step):
        return {"pb": my_a * nk + flipped(my_k, step, nk), "ka": ka}

    def q_copy(source, to, part):
        span = pl.ds(part * piece, piece)
        return pltpu.make_async_remote_copy(
            qd.at[source, :, span], qd.at[source ^ to, :, span],
            q_send.at[source ^ to, part], q_recv.at[source ^ to, part],
            device_id=q_peer(to), device_id_type=MESH)

    def k_copy(source, to, part):
        span = pl.ds(part * piece, piece)
        return pltpu.make_async_remote_copy(
            kv.at[source, :, span], kv.at[source ^ to, :, span],
            k_send.at[source ^ to, part], k_recv.at[source ^ to, part],
            device_id=k_peer(to), device_id_type=MESH)

    def s_copy(to):
        return pltpu.make_async_remote_copy(
            stats.at[0], stats.at[to], s_send.at[to], s_recv.at[to],
            device_id=q_peer(to), device_id_type=MESH)

    def gk_copy(step):
        return pltpu.make_async_remote_copy(
            gk_out.at[step], gk_in.at[step], gk_send.at[step], gk_recv.at[step],
            device_id=k_peer(step), device_id_type=MESH)

    def gk_mid_copy(step):
        return pltpu.make_async_remote_copy(
            gk_out.at[step], gk_mid.at[step ^ 1], gk_send.at[step], gk_mid_recv.at[step ^ 1],
            device_id=k_peer(1), device_id_type=MESH)

    def gq_copy(step):
        return pltpu.make_async_remote_copy(
            gq_out.at[step], gq_in.at[step], gq_send.at[step], gq_recv.at[step],
            device_id=q_peer(step), device_id_type=MESH)

    def gq_mid_copy(step):
        return pltpu.make_async_remote_copy(
            gq_out.at[step], gq_mid.at[step - nka], gq_send.at[step], gq_mid_recv.at[step - nka],
            device_id=q_peer(step - nka), device_id_type=MESH)

    barrier = pltpu.get_barrier_semaphore()
    for step in range(1, nq):
        pl.semaphore_signal(barrier, inc=1, device_id=q_peer(step), device_id_type=MESH)
    for step in range(1, nk):
        pl.semaphore_signal(barrier, inc=1, device_id=k_peer(step), device_id_type=MESH)
    loads = [
        pltpu.make_async_copy(q_ref, qd.at[0, 0], load.at[0]),
        pltpu.make_async_copy(g_ref, qd.at[0, 1], load.at[1]),
        pltpu.make_async_copy(kc_ref, codes.at[0], load.at[2]),
        pltpu.make_async_copy(vc_ref, codes.at[1], load.at[3]),
    ]
    for one in loads:
        one.start()
    for one in loads:
        one.wait()
    kv[0, 0] = (codes[0].astype(WIDE) * key_scale[0]).astype(LOW)
    kv[0, 1] = (codes[1].astype(WIDE) * value_scale[0]).astype(LOW)
    pl.semaphore_wait(barrier, nq + nk - 2)

    def own_copies(part):
        return [
            q_copy(0, nka, part),
            *[k_copy(0, step, part) for step in range(2, nk, 2)],
            k_copy(0, 1, part),
            *[q_copy(0, step, part) for step in range(1, nka)],
        ]

    for part in range(WINDOW):
        for one in own_copies(part):
            one.start()
    top[...] = jnp.full_like(top, -1e30)
    total[...] = jnp.zeros_like(total)
    dot[...] = jnp.zeros_like(dot)
    acc_q[...] = jnp.zeros_like(acc_q)
    acc_k[...] = jnp.zeros_like(acc_k)
    acc_v[...] = jnp.zeros_like(acc_v)

    def serve(part):
        if part + WINDOW < CHUNKS:
            for one, other in zip(own_copies(part), own_copies(part + WINDOW)):
                one.wait_send()
                other.start()
        q_copy(0, nka, part).wait_recv()
        for step in range(1, nka):
            q_copy(nka, step, part).start()
        for step in range(2, nk, 2):
            k_copy(0, step, part).wait_recv()
            k_copy(step, 1, part).start()

    def q_place(u):
        return order(u, nka, nka, 0, subs)

    def k_place(w):
        return order(w, 2, far_w, even_w, subs)

    def first(u, w):
        (j, a), (i, b) = q_place(u), k_place(w)
        span_q, span_k = pl.ds(a * slab, slab), pl.ds(b * slab, slab)
        shape = (slab // 8, 8, slab)
        scores = (contract(kv[i, 0, span_k], qd[j, 0, span_q], (1, 1)) * (factor * log2e)).reshape(shape)
        d_probs = contract(kv[i, 1, span_k], qd[j, 1, span_q], (1, 1))
        old_top = top[u]
        new_top = jnp.maximum(old_top, jnp.max(scores, axis=0))
        shifted = jnp.exp2(scores - new_top[None])
        old = jnp.exp2(old_top - new_top)
        total[u] = total[u] * old + jnp.sum(shifted, axis=0)
        dot[u] = dot[u] * old + jnp.sum(shifted * d_probs.reshape(shape), axis=0)
        top[u] = new_top
        shift[u, i, b] = new_top
        held_e[u, i, span_k] = shifted.reshape(slab, slab)
        held_d[u, i, span_k] = d_probs

    def first_over(us, ws):
        count = len(us) * len(ws)
        if count == 0:
            return

        @pl.loop(0, count, unroll=max(n for n in range(1, UNROLL + 1) if count % n == 0))
        def _(n):
            first(us.start + n // len(ws), ws.start + n % len(ws))

    def forwarded(part):
        for step in range(1, nka):
            q_copy(0, nka + step, part).wait_recv()
        for step in range(3, nk, 2):
            k_copy(0, step, part).wait_recv()

    first_over(range(subs), range(subs))
    for part in range(CHUNKS // 2):
        serve(part)
    for part in range(CHUNKS):
        for step in range(1, nka):
            q_copy(0, step, part).wait_recv()
        k_copy(0, 1, part).wait_recv()
    first_over(range(near_u), range(subs, near_w))
    first_over(range(subs, near_u), range(subs))
    for part in range(CHUNKS // 2, CHUNKS - 1):
        serve(part)
    end_u, end_w, waited = near_u, near_w, 0
    for group in range(subs - 1):
        for part in range(CHUNKS // subs):
            forwarded(waited + part)
        waited += CHUNKS // subs
        first_over(range(end_u), range(end_w, end_w + far_w))
        first_over(range(end_u, end_u + nka), range(end_w + far_w))
        end_u, end_w = end_u + nka, end_w + far_w
    serve(CHUNKS - 1)
    first_over(range(end_u), range(end_w, end_w + even_w))
    first_over(range(end_u, end_u + 1), range(end_w + even_w))
    for part in range(waited, CHUNKS):
        forwarded(part)
    first_over(range(end_u + 1, end_u + nka), range(end_w + far_w))
    first_over(range(end_u + 1), range(end_w + even_w, end_w + far_w))

    count_u = nq * subs
    for u in range(count_u):
        j, a = q_place(u)
        row = q_rank(j) * subs + a
        best = jnp.max(top[u], axis=0, keepdims=True)
        scale = jnp.exp2(top[u] - best)
        whole = jnp.sum(total[u] * scale, axis=0, keepdims=True)
        stats[0, pl.ds(row, 1), :] = best + jnp.log2(whole)
        stats[0, pl.ds(count_u + row, 1), :] = jnp.sum(dot[u] * scale, axis=0, keepdims=True) / whole
    for step in range(nq - 1, 0, -1):
        s_copy(step).start()
    for step in range(1, nq):
        s_copy(step).wait_recv()
    parts = [stats[r, 0:count_u, :] for r in range(nq)]
    best = functools.reduce(jnp.maximum, parts)
    weights = [jnp.exp2(part - best) for part in parts]
    whole = sum(weights)
    lse[...] = best + jnp.log2(whole)
    delta[...] = sum(w * stats[r, count_u : 2 * count_u, :] for r, w in enumerate(weights)) / whole

    def second(u, i):
        j, a = q_place(u)
        span = pl.ds(a * slab, slab)
        row = pl.ds(q_rank(j) * subs + a, 1)
        shape = (slab // 8, 8, slab)
        keys, queries, grads = kv[i, 0], qd[j, 0, span], qd[j, 1, span]
        line, less = lse[row, :], delta[row, :]
        low_p, low_d = [], []
        for b in range(subs):
            span_k = pl.ds(b * slab, slab)
            scale = jnp.exp2(shift[u, i, b] - line)
            probs = held_e[u, i, span_k].reshape(shape) * scale[None]
            d_scores = probs * (held_d[u, i, span_k].reshape(shape) - less[None])
            low_p.append(probs.reshape(slab, slab).astype(LOW))
            low_d.append(d_scores.reshape(slab, slab).astype(LOW))
        probs, d_scores = jnp.concatenate(low_p, axis=0), jnp.concatenate(low_d, axis=0)
        acc_v[i] += contract(probs, grads, (1, 0))
        acc_k[i] += contract(d_scores, queries, (1, 0))
        acc_q[u] += contract(keys, d_scores, (0, 0))

    def second_over(us, steps):
        count = len(us) * len(steps)
        if count == 0:
            return

        @pl.loop(0, count, unroll=max(n for n in range(1, UNROLL + 1) if count % n == 0))
        def _(n):
            second(us.start + n // len(steps), steps.start + n % len(steps) * steps.step)

    def pack_keys(i):
        gk_out[i, 0] = (acc_k[i] * factor).astype(LOW)
        gk_out[i, 1] = acc_v[i].astype(LOW)

    def query_sum(step):
        places = [u for u in range(count_u) if q_place(u)[0] == step]
        return jnp.concatenate([acc_q[u].T for u in places], axis=0) * factor

    everything = range(count_u)
    for i in range(nk - 1, 1, -2):
        second_over(everything, range(i, i + 1))
        pack_keys(i)
        gk_mid_copy(i).start()
    second_over(everything, range(1, 2))
    pack_keys(1)
    if nk < 4:
        gk_copy(1).start()
    second_over(range(near_u, count_u), range(0, nk, 2))
    for step in range(nq - 1, nka, -1):
        gq_out[step] = query_sum(step).astype(LOW)
        gq_mid_copy(step).start()
    far = query_sum(nka)
    second_over(range(near_u), range(2, nk, 2))
    for step in range(1, nka):
        gq_mid_copy(nka + step).wait_recv()
        far = far + gq_mid[step].astype(WIDE)
    gq_out[nka] = far.astype(LOW)
    gq_copy(nka).start()
    for i in range(2, nk, 2):
        gk_mid_copy(i ^ 1).wait_recv()
        gk_out[i, 0] = (acc_k[i] * factor + gk_mid[i, 0].astype(WIDE)).astype(LOW)
        gk_out[i, 1] = (acc_v[i] + gk_mid[i, 1].astype(WIDE)).astype(LOW)
        gk_copy(i).start()
    if nk >= 4:
        gk_copy(1).start()
    second_over(range(near_u), range(0, 1))
    for step in range(nka - 1, 0, -1):
        gq_out[step] = query_sum(step).astype(LOW)
        gq_copy(step).start()

    query_total = query_sum(0)
    for step in range(1, nka + 1):
        gq_copy(step).wait_recv()
        query_total = query_total + gq_in[step].astype(WIDE)
    dq_ref[...] = query_total
    key_sum, value_sum = acc_k[0] * factor, acc_v[0]
    for step in (*range(2, nk, 2), 1):
        gk_copy(step).wait_recv()
        key_sum = key_sum + gk_in[step, 0].astype(WIDE)
        value_sum = value_sum + gk_in[step, 1].astype(WIDE)
    dk_ref[...] = key_sum
    dv_ref[...] = value_sum
    for part in range(CHUNKS):
        if part + WINDOW >= CHUNKS:
            for one in own_copies(part):
                one.wait_send()
        for step in range(1, nka):
            q_copy(nka, step, part).wait_send()
        for step in range(2, nk, 2):
            k_copy(step, 1, part).wait_send()
    for step in range(1, nq):
        s_copy(step).wait_send()
        gq_copy(step).wait_send()
    for step in range(1, nk):
        gk_copy(step).wait_send()


def tail(dq_in, dk_in, dv_in, dq_ref, dk_ref, dv_ref):
    dq_ref[...] = dq_in[...]
    dk_ref[...] = dk_in[...]
    dv_ref[...] = dv_in[...]


def shards(queries, key_codes, value_codes, key_scale, value_scale, out_grad):
    rows, width = queries.shape
    npb, nka = lax.axis_size("pb"), lax.axis_size("ka")
    nq, nk = 2 * nka, npb // 2
    subs = max(rows // 256, 1)
    slab = rows // subs
    vmem = pl.BlockSpec(memory_space=pltpu.VMEM)
    hbm = pl.BlockSpec(memory_space=pltpu.HBM)
    smem = pl.BlockSpec(memory_space=pltpu.SMEM)
    out = jax.ShapeDtypeStruct((rows, width), WIDE)
    counts = (
        (4,), *[(n, CHUNKS) for n in (nq, nq, nk, nk)],
        (nq,), (nq,), (nk,), (nk,), (nk,), (nq,), (nka,), (nq,),
    )
    sems = [pltpu.SemaphoreType.DMA(count) for count in counts]
    places = nq * subs
    grads = pl.pallas_call(
        functools.partial(kernel, nq, nk, nka, subs),
        out_shape=(out, out, out),
        in_specs=[smem, smem, hbm, hbm, hbm, hbm],
        out_specs=(vmem, vmem, vmem),
        scratch_shapes=[
            pltpu.VMEM((nq, 2, rows, width), LOW),
            pltpu.VMEM((nk, 2, rows, width), LOW),
            pltpu.VMEM((2, rows, width), jnp.int32),
            pltpu.VMEM((places, nk, rows, slab), WIDE),
            pltpu.VMEM((places, nk, rows, slab), WIDE),
            pltpu.VMEM((places, nk, subs, 8, slab), WIDE),
            pltpu.VMEM((places, 8, slab), WIDE),
            pltpu.VMEM((places, 8, slab), WIDE),
            pltpu.VMEM((places, 8, slab), WIDE),
            pltpu.VMEM((nq, 2 * places, slab), WIDE),
            pltpu.VMEM((places, slab), WIDE),
            pltpu.VMEM((places, slab), WIDE),
            pltpu.VMEM((places, width, slab), WIDE),
            pltpu.VMEM((nk, rows, width), WIDE),
            pltpu.VMEM((nk, rows, width), WIDE),
            *[pltpu.VMEM((nk, 2, rows, width), LOW)] * 3,
            pltpu.VMEM((nq, rows, width), LOW),
            pltpu.VMEM((nka, rows, width), LOW),
            pltpu.VMEM((nq, rows, width), LOW),
            *sems,
        ],
        compiler_params=pltpu.CompilerParams(
            collective_id=0, has_side_effects=True, vmem_limit_bytes=60 << 20
        ),
    )(key_scale.reshape(1), value_scale.reshape(1), queries, out_grad, key_codes, value_codes)
    return tuple(pl.pallas_call(tail, out_shape=(out, out, out), in_specs=[vmem] * 3, out_specs=(vmem,) * 3)(*grads))


def solution(mesh):
    in_specs = (
        P(("pb", "ka"), "ha"),
        P(("ka", "pb"), "ha"),
        P(("ka", "pb"), "ha"),
        P(),
        P(),
        P(("pb", "ka"), "ha"),
    )
    out_specs = (P(("pb", "ka"), "ha"), P(("ka", "pb"), "ha"), P(("ka", "pb"), "ha"))
    return jax.shard_map(shards, mesh=mesh, in_specs=in_specs, out_specs=out_specs, check_vma=False)
```

```python
import functools
import math

import jax
import jax.numpy as jnp
from jax import lax
from jax.experimental import pallas as pl
from jax.experimental.pallas import tpu as pltpu
from jax.sharding import PartitionSpec as P

MESH = pl.DeviceIdType.MESH
LOW = jnp.bfloat16
EDGES = (0, 2, 4, 7, 8)
CHUNKS = len(EDGES) - 1
WINDOW = 2
UNROLL = 8
WIDE = jnp.float32


def flipped(rank, step, count):
    total = 0
    bit = 1
    while bit < count:
        one = (rank // bit) % 2
        two = (step // bit) % 2
        total = total + bit * (one + two - 2 * one * two)
        bit *= 2
    return total


def contract(left, right, dims):
    return lax.dot_general(left, right, ((dims[:1], dims[1:]), ((), ())), preferred_element_type=WIDE)


def order(index, near, far, evens, subs):
    beside = max(near - 1, 1)
    second, third = index - subs, index - near * subs
    spot = third % max(far, 1)
    if evens:
        spot = 2 * (spot % evens) + spot // evens
    is_second = (second >= 0) * 1 - (third >= 0) * 1
    is_third = (third >= 0) * 1
    step = is_second * (1 + second % beside) + is_third * (near + spot)
    part = (1 - is_second - is_third) * index + is_second * (second // beside) + is_third * (third // max(far, 1))
    return step, part


def kernel(
    nq, nk, nka, subs,
    key_scale, value_scale, q_ref, g_ref, kc_ref, vc_ref,
    dq_ref, dk_ref, dv_ref,
    qd, kv, codes, held_e, held_d, shift, top, total, dot, stats, lse, delta, acc_q, acc_k, acc_v,
    gk_out, gk_mid, gk_in, gk_side, gq_out, gq_mid, gq_in,
    load, q_send, q_recv, k_send, k_recv, s_send, s_recv,
    gk_send, gk_mid_recv, gk_recv, gq_send, gq_mid_recv, gq_recv, side_send, side_recv,
):
    rows, width = q_ref.shape
    slab = rows // subs
    factor = 1.0 / math.sqrt(width)
    log2e = math.log2(math.e)
    pb, ka = lax.axis_index("pb"), lax.axis_index("ka")
    my_a, my_k = pb // nk, pb % nk
    my_q = my_a * nka + ka
    near_u, near_w, far_w, even_w = nka * subs, 2 * subs, nk - 2, nk // 2 - 1

    def q_rank(step):
        return flipped(my_q, step, nq)

    def q_peer(step):
        rank = q_rank(step)
        return {"pb": (rank // nka) * nk + my_k, "ka": rank % nka}

    def k_peer(step):
        return {"pb": my_a * nk + flipped(my_k, step, nk), "ka": ka}

    def chunk(part):
        unit = rows // EDGES[-1]
        return pl.ds(EDGES[part] * unit, (EDGES[part + 1] - EDGES[part]) * unit)

    def q_copy(source, to, part):
        span = chunk(part)
        return pltpu.make_async_remote_copy(
            qd.at[source, :, span], qd.at[source ^ to, :, span],
            q_send.at[source ^ to, part], q_recv.at[source ^ to, part],
            device_id=q_peer(to), device_id_type=MESH)

    def k_copy(source, to, part):
        span = chunk(part)
        return pltpu.make_async_remote_copy(
            kv.at[source, :, span], kv.at[source ^ to, :, span],
            k_send.at[source ^ to, part], k_recv.at[source ^ to, part],
            device_id=k_peer(to), device_id_type=MESH)

    def s_copy(to):
        return pltpu.make_async_remote_copy(
            stats.at[0], stats.at[to], s_send.at[to], s_recv.at[to],
            device_id=q_peer(to), device_id_type=MESH)

    def gk_copy(step, part):
        span = pl.ds(part * slab, slab)
        return pltpu.make_async_remote_copy(
            gk_out.at[step, :, span], gk_in.at[step, :, span], gk_send.at[step, part], gk_recv.at[step, part],
            device_id=k_peer(step), device_id_type=MESH)

    def gk_mid_copy(step, part):
        span = pl.ds(part * slab, slab)
        kinds = pl.ds(0, 1 if part == subs - 1 else 2)
        return pltpu.make_async_remote_copy(
            gk_out.at[step, kinds, span], gk_mid.at[step ^ 1, kinds, span],
            gk_send.at[step, part], gk_mid_recv.at[step ^ 1, part],
            device_id=k_peer(1), device_id_type=MESH)

    def gk_side_copy(step):
        span = pl.ds((subs - 1) * slab, slab)
        return pltpu.make_async_remote_copy(
            gk_out.at[step, 1, span], gk_side.at[step ^ 1], side_send.at[step], side_recv.at[step ^ 1],
            device_id=k_peer(step ^ 1), device_id_type=MESH)

    def gq_copy(step, part):
        span = pl.ds(part * slab, slab)
        return pltpu.make_async_remote_copy(
            gq_out.at[step, span], gq_in.at[step, span], gq_send.at[step, part], gq_recv.at[step, part],
            device_id=q_peer(step), device_id_type=MESH)

    def gq_mid_copy(step, part):
        span = pl.ds(part * slab, slab)
        return pltpu.make_async_remote_copy(
            gq_out.at[step, span], gq_mid.at[step - nka, span],
            gq_send.at[step, part], gq_mid_recv.at[step - nka, part],
            device_id=q_peer(step - nka), device_id_type=MESH)

    barrier = pltpu.get_barrier_semaphore()
    for step in range(1, nq):
        pl.semaphore_signal(barrier, inc=1, device_id=q_peer(step), device_id_type=MESH)
    for step in range(1, nk):
        pl.semaphore_signal(barrier, inc=1, device_id=k_peer(step), device_id_type=MESH)
    loads = [
        pltpu.make_async_copy(q_ref, qd.at[0, 0], load.at[0]),
        pltpu.make_async_copy(g_ref, qd.at[0, 1], load.at[1]),
        pltpu.make_async_copy(kc_ref, codes.at[0], load.at[2]),
        pltpu.make_async_copy(vc_ref, codes.at[1], load.at[3]),
    ]
    for one in loads:
        one.start()
    for one in loads:
        one.wait()
    kv[0, 0] = (codes[0].astype(WIDE) * key_scale[0]).astype(LOW)
    kv[0, 1] = (codes[1].astype(WIDE) * value_scale[0]).astype(LOW)
    pl.semaphore_wait(barrier, nq + nk - 2)

    def own_copies(part):
        return [
            q_copy(0, nka, part),
            *[k_copy(0, step, part) for step in range(2, nk, 2)],
            k_copy(0, 1, part),
            *[q_copy(0, step, part) for step in range(1, nka)],
        ]

    for part in range(WINDOW):
        for one in own_copies(part):
            one.start()
    top[...] = jnp.full_like(top, -1e30)
    total[...] = jnp.zeros_like(total)
    dot[...] = jnp.zeros_like(dot)
    acc_q[...] = jnp.zeros_like(acc_q)
    acc_k[...] = jnp.zeros_like(acc_k)
    acc_v[...] = jnp.zeros_like(acc_v)

    def serve(part):
        if part + WINDOW < CHUNKS:
            for one, other in zip(own_copies(part), own_copies(part + WINDOW)):
                one.wait_send()
                other.start()
        q_copy(0, nka, part).wait_recv()
        for step in range(1, nka):
            q_copy(nka, step, part).start()
        for step in range(2, nk, 2):
            k_copy(0, step, part).wait_recv()
            k_copy(step, 1, part).start()

    def q_place(u):
        return order(u, nka, nka, 0, subs)

    def k_place(w):
        return order(w, 2, far_w, even_w, subs)

    def first(u, w):
        (j, a), (i, b) = q_place(u), k_place(w)
        span_q, span_k = pl.ds(a * slab, slab), pl.ds(b * slab, slab)
        shape = (slab // 8, 8, slab)
        scores = (contract(kv[i, 0, span_k], qd[j, 0, span_q], (1, 1)) * (factor * log2e)).reshape(shape)
        d_probs = contract(kv[i, 1, span_k], qd[j, 1, span_q], (1, 1))
        old_top = top[u]
        new_top = jnp.maximum(old_top, jnp.max(scores, axis=0))
        shifted = jnp.exp2(scores - new_top[None])
        old = jnp.exp2(old_top - new_top)
        total[u] = total[u] * old + jnp.sum(shifted, axis=0)
        dot[u] = dot[u] * old + jnp.sum(shifted * d_probs.reshape(shape), axis=0)
        top[u] = new_top
        shift[u, i, b] = new_top
        held_e[u, i, span_k] = shifted.reshape(slab, slab)
        held_d[u, i, span_k] = d_probs

    def first_over(us, ws):
        count = len(us) * len(ws)
        if count == 0:
            return

        @pl.loop(0, count, unroll=max(n for n in range(1, UNROLL + 1) if count % n == 0))
        def _(n):
            first(us.start + n // len(ws), ws.start + n % len(ws))

    first_over(range(subs), range(subs))
    end_u, end_w, served, share = subs, subs, 0, CHUNKS // subs
    for group in range(subs):
        while served < max(1, (group + 1) * share - WINDOW):
            serve(served)
            served += 1
        for part in range(group * share, (group + 1) * share):
            for step in range(1, nka):
                q_copy(0, step, part).wait_recv()
            k_copy(0, 1, part).wait_recv()
        first_over(range(end_u), range(end_w, end_w + 1))
        first_over(range(end_u, end_u + nka - 1), range(end_w + 1))
        end_u, end_w = end_u + nka - 1, end_w + 1
    for group in range(subs):
        while served < (group + 1) * share:
            serve(served)
            served += 1
        first_over(range(end_u), range(end_w, end_w + even_w))
        first_over(range(end_u, end_u + 1), range(end_w + even_w))
        if served < CHUNKS:
            serve(served)
            served += 1
        for part in range(group * share, (group + 1) * share):
            for step in range(1, nka):
                q_copy(0, nka + step, part).wait_recv()
        first_over(range(end_u + 1, end_u + nka), range(end_w + even_w))
        for part in range(group * share, (group + 1) * share):
            for step in range(3, nk, 2):
                k_copy(0, step, part).wait_recv()
        first_over(range(end_u + nka), range(end_w + even_w, end_w + far_w))
        end_u, end_w = end_u + nka, end_w + far_w

    count_u = nq * subs
    for u in range(count_u):
        j, a = q_place(u)
        row = q_rank(j) * subs + a
        best = jnp.max(top[u], axis=0, keepdims=True)
        scale = jnp.exp2(top[u] - best)
        whole = jnp.sum(total[u] * scale, axis=0, keepdims=True)
        stats[0, pl.ds(row, 1), :] = best + jnp.log2(whole)
        stats[0, pl.ds(count_u + row, 1), :] = jnp.sum(dot[u] * scale, axis=0, keepdims=True) / whole
    for step in range(nq - 1, 0, -1):
        s_copy(step).start()
    for step in range(1, nq):
        s_copy(step).wait_recv()
    parts = [stats[r, 0:count_u, :] for r in range(nq)]
    best = functools.reduce(jnp.maximum, parts)
    weights = [jnp.exp2(part - best) for part in parts]
    whole = sum(weights)
    lse[...] = best + jnp.log2(whole)
    delta[...] = sum(w * stats[r, count_u : 2 * count_u, :] for r, w in enumerate(weights)) / whole

    def second(u, p):
        j, a = q_place(u)
        i, b = turn(p)
        span, span_k = pl.ds(a * slab, slab), pl.ds(b * slab, slab)
        row = pl.ds(q_rank(j) * subs + a, 1)
        shape = (slab // 8, 8, slab)
        queries, grads = qd[j, 0, span], qd[j, 1, span]
        scale = jnp.exp2(shift[u, i, b] - lse[row, :])
        probs = held_e[u, i, span_k].reshape(shape) * scale[None]
        d_scores = probs * (held_d[u, i, span_k].reshape(shape) - delta[row, :][None])
        d_scores = d_scores.reshape(slab, slab).astype(LOW)
        acc_v[i, span_k] += contract(probs.reshape(slab, slab).astype(LOW), grads, (1, 0))
        acc_k[i, span_k] += contract(d_scores, queries, (1, 0))
        acc_q[u] += contract(kv[i, 0, span_k], d_scores, (0, 0))

    def turn(p):
        nth = p // subs
        odd, early = (nth < even_w) * 1, (nth < 2 * even_w) * 1
        even = (early - odd) * 2 * (nth - even_w + 1) + (1 - early) * (nk - 1 - nth)
        return odd * (nk - 1 - 2 * nth) + even, p % subs

    def second_over(us, ps):
        count = len(us) * len(ps)
        if count == 0:
            return

        @pl.loop(0, count, unroll=max(n for n in range(1, UNROLL + 1) if count % n == 0))
        def _(n):
            second(us.start + n // len(ps), ps.start + n % len(ps))

    def pack_keys(i, b):
        span = pl.ds(b * slab, slab)
        gk_out[i, 0, span] = (acc_k[i, span] * factor).astype(LOW)
        gk_out[i, 1, span] = acc_v[i, span].astype(LOW)

    def query_part(u):
        return acc_q[u].T * factor

    def send_queries(u):
        j, a = q_place(u)
        gq_out[j, pl.ds(a * slab, slab)] = query_part(u).astype(LOW)
        (gq_mid_copy if j > nka else gq_copy)(j, a).start()

    def send_far(u):
        _, a = q_place(u)
        span = pl.ds(a * slab, slab)
        far = query_part(u)
        for step in range(1, nka):
            gq_mid_copy(nka + step, a).wait_recv()
            far = far + gq_mid[step, span].astype(WIDE)
        gq_out[nka, span] = far.astype(LOW)
        gq_copy(nka, a).start()

    last, mids = nk * subs, even_w * subs
    beside = last - 2 * subs
    for p in range(mids):
        second_over(range(count_u), range(p, p + 1))
        i, b = turn(p)
        pack_keys(i, b)
        gk_mid_copy(i, b).start()
        if b == subs - 1:
            gk_side_copy(i).start()
    for group in range(subs):
        begin = near_u + group * nka
        second_over(range(begin + 1, begin + nka), range(mids, last))
        for u in range(begin + 1, begin + nka):
            send_queries(u)

    def send_even(b):
        span = pl.ds(b * slab, slab)
        for i in range(2, nk, 2):
            gk_mid_copy(i ^ 1, b).wait_recv()
            gk_out[i, 0, span] = (acc_k[i, span] * factor + gk_mid[i, 0, span].astype(WIDE)).astype(LOW)
            value_sum = acc_v[i, span]
            if b < subs - 1:
                value_sum = value_sum + gk_mid[i, 1, span].astype(WIDE)
            gk_out[i, 1, span] = value_sum.astype(LOW)
            gk_copy(i, b).start()

    second_over(range(near_u), range(mids, beside))
    for group in range(subs):
        second_over(range(near_u + group * nka, near_u + group * nka + 1), range(mids, last))
    for b in range(subs - 1):
        send_even(b)
        send_far(near_u + b * nka)
    second_over(range(near_u), range(beside, beside + subs))
    for b in range(subs):
        pack_keys(1, b)
        if b == subs - 1 and nk > 2:
            span = pl.ds(b * slab, slab)
            value_sum = acc_v[1, span]
            for i in range(2, nk, 2):
                gk_side_copy(i ^ 1).wait_recv()
                value_sum = value_sum + gk_side[i].astype(WIDE)
            gk_out[1, 1, span] = value_sum.astype(LOW)
        gk_copy(1, b).start()
    send_even(subs - 1)
    send_far(near_u + (subs - 1) * nka)
    second_over(range(subs, near_u), range(last - subs, last))
    for u in range(subs, near_u):
        send_queries(u)
    second_over(range(subs), range(last - subs, last))

    for a in range(subs):
        span = pl.ds(a * slab, slab)
        query_total = query_part(a)
        for step in range(1, nka + 1):
            gq_copy(step, a).wait_recv()
            query_total = query_total + gq_in[step, span].astype(WIDE)
        dq_ref[span, :] = query_total
    for b in range(subs):
        span = pl.ds(b * slab, slab)
        key_sum, value_sum = acc_k[0, span] * factor, acc_v[0, span]
        for step in (*range(2, nk, 2), 1):
            gk_copy(step, b).wait_recv()
            key_sum = key_sum + gk_in[step, 0, span].astype(WIDE)
            value_sum = value_sum + gk_in[step, 1, span].astype(WIDE)
        dk_ref[span, :] = key_sum
        dv_ref[span, :] = value_sum
    for part in range(CHUNKS):
        if part + WINDOW >= CHUNKS:
            for one in own_copies(part):
                one.wait_send()
        for step in range(1, nka):
            q_copy(nka, step, part).wait_send()
        for step in range(2, nk, 2):
            k_copy(step, 1, part).wait_send()
    for step in range(1, nq):
        s_copy(step).wait_send()
        for part in range(subs):
            gq_copy(step, part).wait_send()
    for step in range(1, nk):
        relayed = step > 1 and step % 2 == 1
        for part in range(subs):
            (gk_mid_copy if relayed else gk_copy)(step, part).wait_send()
        if relayed:
            gk_side_copy(step).wait_send()


def tail(dq_in, dk_in, dv_in, dq_ref, dk_ref, dv_ref):
    dq_ref[...] = dq_in[...]
    dk_ref[...] = dk_in[...]
    dv_ref[...] = dv_in[...]


def shards(queries, key_codes, value_codes, key_scale, value_scale, out_grad):
    rows, width = queries.shape
    npb, nka = lax.axis_size("pb"), lax.axis_size("ka")
    nq, nk = 2 * nka, npb // 2
    subs = max(rows // 256, 1)
    slab = rows // subs
    vmem = pl.BlockSpec(memory_space=pltpu.VMEM)
    hbm = pl.BlockSpec(memory_space=pltpu.HBM)
    smem = pl.BlockSpec(memory_space=pltpu.SMEM)
    out = jax.ShapeDtypeStruct((rows, width), WIDE)
    counts = (
        (4,), *[(n, CHUNKS) for n in (nq, nq, nk, nk)],
        (nq,), (nq,), *[(n, subs) for n in (nk, nk, nk, nq, nka, nq)], (nk,), (nk,),
    )
    sems = [pltpu.SemaphoreType.DMA(count) for count in counts]
    places = nq * subs
    grads = pl.pallas_call(
        functools.partial(kernel, nq, nk, nka, subs),
        out_shape=(out, out, out),
        in_specs=[smem, smem, hbm, hbm, hbm, hbm],
        out_specs=(vmem, vmem, vmem),
        scratch_shapes=[
            pltpu.VMEM((nq, 2, rows, width), LOW),
            pltpu.VMEM((nk, 2, rows, width), LOW),
            pltpu.VMEM((2, rows, width), jnp.int32),
            pltpu.VMEM((places, nk, rows, slab), WIDE),
            pltpu.VMEM((places, nk, rows, slab), WIDE),
            pltpu.VMEM((places, nk, subs, 8, slab), WIDE),
            pltpu.VMEM((places, 8, slab), WIDE),
            pltpu.VMEM((places, 8, slab), WIDE),
            pltpu.VMEM((places, 8, slab), WIDE),
            pltpu.VMEM((nq, 2 * places, slab), WIDE),
            pltpu.VMEM((places, slab), WIDE),
            pltpu.VMEM((places, slab), WIDE),
            pltpu.VMEM((places, width, slab), WIDE),
            pltpu.VMEM((nk, rows, width), WIDE),
            pltpu.VMEM((nk, rows, width), WIDE),
            *[pltpu.VMEM((nk, 2, rows, width), LOW)] * 3,
            pltpu.VMEM((nk, slab, width), LOW),
            pltpu.VMEM((nq, rows, width), LOW),
            pltpu.VMEM((nka, rows, width), LOW),
            pltpu.VMEM((nq, rows, width), LOW),
            *sems,
        ],
        compiler_params=pltpu.CompilerParams(
            collective_id=0, has_side_effects=True, vmem_limit_bytes=60 << 20
        ),
    )(key_scale.reshape(1), value_scale.reshape(1), queries, out_grad, key_codes, value_codes)
    return tuple(pl.pallas_call(tail, out_shape=(out, out, out), in_specs=[vmem] * 3, out_specs=(vmem,) * 3)(*grads))


def solution(mesh):
    in_specs = (
        P(("pb", "ka"), "ha"),
        P(("ka", "pb"), "ha"),
        P(("ka", "pb"), "ha"),
        P(),
        P(),
        P(("pb", "ka"), "ha"),
    )
    out_specs = (P(("pb", "ka"), "ha"), P(("ka", "pb"), "ha"), P(("ka", "pb"), "ha"))
    return jax.shard_map(shards, mesh=mesh, in_specs=in_specs, out_specs=out_specs, check_vma=False)
```

```python
import functools
import math

import jax
import jax.numpy as jnp
from jax import lax
from jax.experimental import pallas as pl
from jax.experimental.pallas import tpu as pltpu
from jax.sharding import PartitionSpec as P

MESH = pl.DeviceIdType.MESH
LOW = jnp.bfloat16
EDGES = (0, 2, 4, 7, 8)
CHUNKS = len(EDGES) - 1
WINDOW = 2
UNROLL = 13
WIDE = jnp.float32


def flipped(rank, step, count):
    total = 0
    bit = 1
    while bit < count:
        one = (rank // bit) % 2
        two = (step // bit) % 2
        total = total + bit * (one + two - 2 * one * two)
        bit *= 2
    return total


def contract(left, right, dims):
    return lax.dot_general(left, right, ((dims[:1], dims[1:]), ((), ())), preferred_element_type=WIDE)


def order(index, near, far, evens, subs):
    beside = max(near - 1, 1)
    second, third = index - subs, index - near * subs
    spot = third % max(far, 1)
    if evens:
        spot = 2 * (spot % evens) + spot // evens
    is_second = (second >= 0) * 1 - (third >= 0) * 1
    is_third = (third >= 0) * 1
    step = is_second * (1 + second % beside) + is_third * (near + spot)
    part = (1 - is_second - is_third) * index + is_second * (second // beside) + is_third * (third // max(far, 1))
    return step, part


def kernel(
    nq, nk, nka, subs,
    key_scale, value_scale, q_ref, g_ref, kc_ref, vc_ref,
    dq_hbm, dk_hbm, dv_hbm,
    dq_ref, dk_ref, dv_ref, leave, qd, kv, codes, held_e, held_d, shift, top, total, dot, stats, lse, delta, acc_q, acc_k, acc_v,
    gk_out, gk_mid, gk_in, gk_side, gq_out, gq_mid, gq_in,
    load, q_send, q_recv, k_send, k_recv, s_send, s_recv,
    gk_send, gk_mid_recv, gk_recv, gq_send, gq_mid_recv, gq_recv, side_send, side_recv,
):
    rows, width = q_ref.shape
    slab = rows // subs
    factor = 1.0 / math.sqrt(width)
    log2e = math.log2(math.e)
    pb, ka = lax.axis_index("pb"), lax.axis_index("ka")
    my_a, my_k = pb // nk, pb % nk
    my_q = my_a * nka + ka
    near_u, near_w, far_w, even_w = nka * subs, 2 * subs, nk - 2, nk // 2 - 1

    def q_rank(step):
        return flipped(my_q, step, nq)

    def q_peer(step):
        rank = q_rank(step)
        return {"pb": (rank // nka) * nk + my_k, "ka": rank % nka}

    def k_peer(step):
        return {"pb": my_a * nk + flipped(my_k, step, nk), "ka": ka}

    def chunk(part):
        unit = rows // EDGES[-1]
        return pl.ds(EDGES[part] * unit, (EDGES[part + 1] - EDGES[part]) * unit)

    def q_copy(source, to, part):
        span = chunk(part)
        return pltpu.make_async_remote_copy(
            qd.at[source, :, span], qd.at[source ^ to, :, span],
            q_send.at[source ^ to, part], q_recv.at[source ^ to, part],
            device_id=q_peer(to), device_id_type=MESH)

    def k_copy(source, to, part):
        span = chunk(part)
        return pltpu.make_async_remote_copy(
            kv.at[source, :, span], kv.at[source ^ to, :, span],
            k_send.at[source ^ to, part], k_recv.at[source ^ to, part],
            device_id=k_peer(to), device_id_type=MESH)

    def s_copy(to):
        return pltpu.make_async_remote_copy(
            stats.at[0], stats.at[to], s_send.at[to], s_recv.at[to],
            device_id=q_peer(to), device_id_type=MESH)

    def gk_copy(step, part):
        span = pl.ds(part * slab, slab)
        return pltpu.make_async_remote_copy(
            gk_out.at[step, :, span], gk_in.at[step, :, span], gk_send.at[step, part], gk_recv.at[step, part],
            device_id=k_peer(step), device_id_type=MESH)

    def gk_mid_copy(step, part):
        span = pl.ds(part * slab, slab)
        kinds = pl.ds(0, 1 if part == subs - 1 else 2)
        return pltpu.make_async_remote_copy(
            gk_out.at[step, kinds, span], gk_mid.at[step ^ 1, kinds, span],
            gk_send.at[step, part], gk_mid_recv.at[step ^ 1, part],
            device_id=k_peer(1), device_id_type=MESH)

    def gk_side_copy(step):
        span = pl.ds((subs - 1) * slab, slab)
        return pltpu.make_async_remote_copy(
            gk_out.at[step, 1, span], gk_side.at[step ^ 1], side_send.at[step], side_recv.at[step ^ 1],
            device_id=k_peer(step ^ 1), device_id_type=MESH)

    def gq_copy(step, part):
        span = pl.ds(part * slab, slab)
        return pltpu.make_async_remote_copy(
            gq_out.at[step, span], gq_in.at[step, span], gq_send.at[step, part], gq_recv.at[step, part],
            device_id=q_peer(step), device_id_type=MESH)

    def gq_mid_copy(step, part):
        span = pl.ds(part * slab, slab)
        return pltpu.make_async_remote_copy(
            gq_out.at[step, span], gq_mid.at[step - nka, span],
            gq_send.at[step, part], gq_mid_recv.at[step - nka, part],
            device_id=q_peer(step - nka), device_id_type=MESH)

    barrier = pltpu.get_barrier_semaphore()
    for step in range(1, nq):
        pl.semaphore_signal(barrier, inc=1, device_id=q_peer(step), device_id_type=MESH)
    for step in range(1, nk):
        pl.semaphore_signal(barrier, inc=1, device_id=k_peer(step), device_id_type=MESH)
    loads = [
        pltpu.make_async_copy(q_ref, qd.at[0, 0], load.at[0]),
        pltpu.make_async_copy(g_ref, qd.at[0, 1], load.at[1]),
        pltpu.make_async_copy(kc_ref, codes.at[0], load.at[2]),
        pltpu.make_async_copy(vc_ref, codes.at[1], load.at[3]),
    ]
    for one in loads:
        one.start()
    for one in loads:
        one.wait()
    kv[0, 0] = (codes[0].astype(WIDE) * key_scale[0]).astype(LOW)
    kv[0, 1] = (codes[1].astype(WIDE) * value_scale[0]).astype(LOW)
    pl.semaphore_wait(barrier, nq + nk - 2)

    def own_copies(part):
        return [
            *[k_copy(0, step, part) for step in range(2, nk, 2)],
            q_copy(0, nka, part),
            k_copy(0, 1, part),
            *[q_copy(0, step, part) for step in range(1, nka)],
        ]

    for part in range(WINDOW):
        for one in own_copies(part):
            one.start()
    top[...] = jnp.full_like(top, -1e30)
    total[...] = jnp.zeros_like(total)
    dot[...] = jnp.zeros_like(dot)
    acc_q[...] = jnp.zeros_like(acc_q)
    acc_k[...] = jnp.zeros_like(acc_k)
    acc_v[...] = jnp.zeros_like(acc_v)

    def serve(part):
        if part + WINDOW < CHUNKS:
            for one, other in zip(own_copies(part), own_copies(part + WINDOW)):
                one.wait_send()
                other.start()
        q_copy(0, nka, part).wait_recv()
        for step in range(1, nka):
            q_copy(nka, step, part).start()
        for step in range(2, nk, 2):
            k_copy(0, step, part).wait_recv()
            k_copy(step, 1, part).start()

    def q_place(u):
        return order(u, nka, nka, 0, subs)

    def k_place(w):
        return order(w, 2, far_w, even_w, subs)

    def first(u, w):
        (j, a), (i, b) = q_place(u), k_place(w)
        span_q, span_k = pl.ds(a * slab, slab), pl.ds(b * slab, slab)
        shape = (slab // 8, 8, slab)
        scores = (contract(kv[i, 0, span_k], qd[j, 0, span_q], (1, 1)) * (factor * log2e)).reshape(shape)
        d_probs = contract(kv[i, 1, span_k], qd[j, 1, span_q], (1, 1))
        old_top = top[u]
        new_top = jnp.maximum(old_top, jnp.max(scores, axis=0))
        shifted = jnp.exp2(scores - new_top[None])
        old = jnp.exp2(old_top - new_top)
        total[u] = total[u] * old + jnp.sum(shifted, axis=0)
        dot[u] = dot[u] * old + jnp.sum(shifted * d_probs.reshape(shape), axis=0)
        top[u] = new_top
        shift[u, i, b] = new_top
        held_e[u, i, span_k] = shifted.reshape(slab, slab)
        held_d[u, i, span_k] = d_probs

    def first_over(us, ws):
        count = len(us) * len(ws)
        if count == 0:
            return

        @pl.loop(0, count, unroll=max(n for n in range(1, UNROLL + 1) if count % n == 0))
        def _(n):
            first(us.start + n // len(ws), ws.start + n % len(ws))

    first_over(range(subs), range(subs))
    end_u, end_w, served, share = subs, subs, 0, CHUNKS // subs
    for group in range(subs):
        while served < max(1, (group + 1) * share - WINDOW):
            serve(served)
            served += 1
        for part in range(group * share, (group + 1) * share):
            for step in range(1, nka):
                q_copy(0, step, part).wait_recv()
            k_copy(0, 1, part).wait_recv()
        first_over(range(end_u), range(end_w, end_w + 1))
        first_over(range(end_u, end_u + nka - 1), range(end_w + 1))
        end_u, end_w = end_u + nka - 1, end_w + 1
    for group in range(subs):
        while served < (group + 1) * share:
            serve(served)
            served += 1
        first_over(range(end_u), range(end_w, end_w + even_w))
        first_over(range(end_u, end_u + 1), range(end_w + even_w))
        if served < CHUNKS:
            serve(served)
            served += 1
        for part in range(group * share, (group + 1) * share):
            for step in range(1, nka):
                q_copy(0, nka + step, part).wait_recv()
        first_over(range(end_u + 1, end_u + nka), range(end_w + even_w))
        for part in range(group * share, (group + 1) * share):
            for step in range(3, nk, 2):
                k_copy(0, step, part).wait_recv()
        first_over(range(end_u + nka), range(end_w + even_w, end_w + far_w))
        end_u, end_w = end_u + nka, end_w + far_w

    count_u = nq * subs
    for u in range(count_u):
        j, a = q_place(u)
        row = q_rank(j) * subs + a
        best = jnp.max(top[u], axis=0, keepdims=True)
        scale = jnp.exp2(top[u] - best)
        whole = jnp.sum(total[u] * scale, axis=0, keepdims=True)
        stats[0, pl.ds(row, 1), :] = best + jnp.log2(whole)
        stats[0, pl.ds(count_u + row, 1), :] = jnp.sum(dot[u] * scale, axis=0, keepdims=True) / whole
    for step in range(nq - 1, 0, -1):
        s_copy(step).start()
    for step in range(1, nq):
        s_copy(step).wait_recv()
    parts = [stats[r, 0:count_u, :] for r in range(nq)]
    best = functools.reduce(jnp.maximum, parts)
    weights = [jnp.exp2(part - best) for part in parts]
    whole = sum(weights)
    lse[...] = best + jnp.log2(whole)
    delta[...] = sum(w * stats[r, count_u : 2 * count_u, :] for r, w in enumerate(weights)) / whole

    def second(u, p):
        j, a = q_place(u)
        i, b = turn(p)
        span, span_k = pl.ds(a * slab, slab), pl.ds(b * slab, slab)
        row = pl.ds(q_rank(j) * subs + a, 1)
        shape = (slab // 8, 8, slab)
        queries, grads = qd[j, 0, span], qd[j, 1, span]
        scale = jnp.exp2(shift[u, i, b] - lse[row, :])
        probs = held_e[u, i, span_k].reshape(shape) * scale[None]
        d_scores = probs * (held_d[u, i, span_k].reshape(shape) - delta[row, :][None])
        d_scores = d_scores.reshape(slab, slab).astype(LOW)
        acc_v[i, span_k] += contract(probs.reshape(slab, slab).astype(LOW), grads, (1, 0))
        acc_k[i, span_k] += contract(d_scores, queries, (1, 0))
        acc_q[u] += contract(kv[i, 0, span_k], d_scores, (0, 0))

    def turn(p):
        nth = p // subs
        odd, early = (nth < even_w) * 1, (nth < 2 * even_w) * 1
        even = (early - odd) * 2 * (nth - even_w + 1) + (1 - early) * (nk - 1 - nth)
        return odd * (nk - 1 - 2 * nth) + even, p % subs

    def second_over(us, ps):
        count = len(us) * len(ps)
        if count == 0:
            return

        @pl.loop(0, count, unroll=max(n for n in range(1, UNROLL + 1) if count % n == 0))
        def _(n):
            second(us.start + n // len(ps), ps.start + n % len(ps))

    def pack_keys(i, b):
        span = pl.ds(b * slab, slab)
        gk_out[i, 0, span] = (acc_k[i, span] * factor).astype(LOW)
        gk_out[i, 1, span] = acc_v[i, span].astype(LOW)

    def query_part(u):
        return acc_q[u].T * factor

    def send_queries(u):
        j, a = q_place(u)
        gq_out[j, pl.ds(a * slab, slab)] = query_part(u).astype(LOW)
        (gq_mid_copy if j > nka else gq_copy)(j, a).start()

    def send_far(u):
        _, a = q_place(u)
        span = pl.ds(a * slab, slab)
        far = query_part(u)
        for step in range(1, nka):
            gq_mid_copy(nka + step, a).wait_recv()
            far = far + gq_mid[step, span].astype(WIDE)
        gq_out[nka, span] = far.astype(LOW)
        gq_copy(nka, a).start()

    last, mids = nk * subs, even_w * subs
    beside = last - 2 * subs
    for p in range(mids):
        second_over(range(count_u), range(p, p + 1))
        i, b = turn(p)
        pack_keys(i, b)
        gk_mid_copy(i, b).start()
        if b == subs - 1:
            gk_side_copy(i).start()
    for group in range(subs):
        begin = near_u + group * nka
        second_over(range(begin + 1, begin + nka), range(mids, last))
        for u in range(begin + 1, begin + nka):
            send_queries(u)

    def send_even(b):
        span = pl.ds(b * slab, slab)
        for i in range(2, nk, 2):
            gk_mid_copy(i ^ 1, b).wait_recv()
            gk_out[i, 0, span] = (acc_k[i, span] * factor + gk_mid[i, 0, span].astype(WIDE)).astype(LOW)
            value_sum = acc_v[i, span]
            if b < subs - 1:
                value_sum = value_sum + gk_mid[i, 1, span].astype(WIDE)
            gk_out[i, 1, span] = value_sum.astype(LOW)
            gk_copy(i, b).start()

    second_over(range(near_u), range(mids, beside))
    for group in range(subs):
        second_over(range(near_u + group * nka, near_u + group * nka + 1), range(mids, last))
    for b in range(subs - 1):
        send_even(b)
        send_far(near_u + b * nka)
    second_over(range(near_u), range(beside, beside + subs))
    for b in range(subs):
        pack_keys(1, b)
        if b == subs - 1 and nk > 2:
            span = pl.ds(b * slab, slab)
            value_sum = acc_v[1, span]
            for i in range(2, nk, 2):
                gk_side_copy(i ^ 1).wait_recv()
                value_sum = value_sum + gk_side[i].astype(WIDE)
            gk_out[1, 1, span] = value_sum.astype(LOW)
        gk_copy(1, b).start()
    send_even(subs - 1)
    send_far(near_u + (subs - 1) * nka)
    second_over(range(subs, near_u), range(last - subs, last))
    for u in range(subs, near_u):
        send_queries(u)
    second_over(range(subs), range(last - subs, last))

    def out_copy(n, part):
        span = pl.ds(part * slab, slab)
        source, target = ((dq_ref, dq_hbm), (dk_ref, dk_hbm), (dv_ref, dv_hbm))[n]
        return pltpu.make_async_copy(source.at[span], target.at[span], leave.at[n, part])

    for a in range(subs):
        span = pl.ds(a * slab, slab)
        query_total = query_part(a)
        for step in range(1, nka + 1):
            gq_copy(step, a).wait_recv()
            query_total = query_total + gq_in[step, span].astype(WIDE)
        dq_ref[span, :] = query_total
        out_copy(0, a).start()
    for b in range(subs):
        span = pl.ds(b * slab, slab)
        key_sum, value_sum = acc_k[0, span] * factor, acc_v[0, span]
        for step in (*range(2, nk, 2), 1):
            gk_copy(step, b).wait_recv()
            key_sum = key_sum + gk_in[step, 0, span].astype(WIDE)
            value_sum = value_sum + gk_in[step, 1, span].astype(WIDE)
        dk_ref[span, :] = key_sum
        dv_ref[span, :] = value_sum
        out_copy(1, b).start()
        out_copy(2, b).start()
    for part in range(CHUNKS):
        if part + WINDOW >= CHUNKS:
            for one in own_copies(part):
                one.wait_send()
        for step in range(1, nka):
            q_copy(nka, step, part).wait_send()
        for step in range(2, nk, 2):
            k_copy(step, 1, part).wait_send()
    for step in range(1, nq):
        s_copy(step).wait_send()
        for part in range(subs):
            gq_copy(step, part).wait_send()
    for step in range(1, nk):
        relayed = step > 1 and step % 2 == 1
        for part in range(subs):
            (gk_mid_copy if relayed else gk_copy)(step, part).wait_send()
        if relayed:
            gk_side_copy(step).wait_send()
    for n in range(3):
        for part in range(subs):
            out_copy(n, part).wait()


def tail(dq_in, dk_in, dv_in, dq_ref, dk_ref, dv_ref):
    dq_ref[...] = dq_in[...]
    dk_ref[...] = dk_in[...]
    dv_ref[...] = dv_in[...]


def shards(queries, key_codes, value_codes, key_scale, value_scale, out_grad):
    rows, width = queries.shape
    npb, nka = lax.axis_size("pb"), lax.axis_size("ka")
    nq, nk = 2 * nka, npb // 2
    subs = max(rows // 256, 1)
    slab = rows // subs
    vmem = pl.BlockSpec(memory_space=pltpu.VMEM)
    hbm = pl.BlockSpec(memory_space=pltpu.HBM)
    smem = pl.BlockSpec(memory_space=pltpu.SMEM)
    out = jax.ShapeDtypeStruct((rows, width), WIDE)
    counts = (
        (4,), *[(n, CHUNKS) for n in (nq, nq, nk, nk)],
        (nq,), (nq,), *[(n, subs) for n in (nk, nk, nk, nq, nka, nq)], (nk,), (nk,),
    )
    sems = [pltpu.SemaphoreType.DMA(count) for count in counts]
    places = nq * subs
    grads = pl.pallas_call(
        functools.partial(kernel, nq, nk, nka, subs),
        out_shape=(out, out, out),
        in_specs=[smem, smem, hbm, hbm, hbm, hbm],
        out_specs=(hbm, hbm, hbm),
        scratch_shapes=[
            *[pltpu.VMEM((rows, width), WIDE)] * 3,
            pltpu.SemaphoreType.DMA((3, subs)),
            pltpu.VMEM((nq, 2, rows, width), LOW),
            pltpu.VMEM((nk, 2, rows, width), LOW),
            pltpu.VMEM((2, rows, width), jnp.int32),
            pltpu.VMEM((places, nk, rows, slab), WIDE),
            pltpu.VMEM((places, nk, rows, slab), WIDE),
            pltpu.VMEM((places, nk, subs, 8, slab), WIDE),
            pltpu.VMEM((places, 8, slab), WIDE),
            pltpu.VMEM((places, 8, slab), WIDE),
            pltpu.VMEM((places, 8, slab), WIDE),
            pltpu.VMEM((nq, 2 * places, slab), WIDE),
            pltpu.VMEM((places, slab), WIDE),
            pltpu.VMEM((places, slab), WIDE),
            pltpu.VMEM((places, width, slab), WIDE),
            pltpu.VMEM((nk, rows, width), WIDE),
            pltpu.VMEM((nk, rows, width), WIDE),
            *[pltpu.VMEM((nk, 2, rows, width), LOW)] * 3,
            pltpu.VMEM((nk, slab, width), LOW),
            pltpu.VMEM((nq, rows, width), LOW),
            pltpu.VMEM((nka, rows, width), LOW),
            pltpu.VMEM((nq, rows, width), LOW),
            *sems,
        ],
        compiler_params=pltpu.CompilerParams(
            collective_id=0, has_side_effects=True, vmem_limit_bytes=60 << 20
        ),
    )(key_scale.reshape(1), value_scale.reshape(1), queries, out_grad, key_codes, value_codes)
    return tuple(pl.pallas_call(tail, out_shape=(out, out, out), in_specs=[vmem] * 3, out_specs=(vmem,) * 3)(*grads))


def solution(mesh):
    in_specs = (
        P(("pb", "ka"), "ha"),
        P(("ka", "pb"), "ha"),
        P(("ka", "pb"), "ha"),
        P(),
        P(),
        P(("pb", "ka"), "ha"),
    )
    out_specs = (P(("pb", "ka"), "ha"), P(("ka", "pb"), "ha"), P(("ka", "pb"), "ha"))
    return jax.shard_map(shards, mesh=mesh, in_specs=in_specs, out_specs=out_specs, check_vma=False)
```

```python
import functools
import math

import jax
import jax.numpy as jnp
from jax import lax
from jax.experimental import pallas as pl
from jax.experimental.pallas import tpu as pltpu
from jax.sharding import PartitionSpec as P

MESH = pl.DeviceIdType.MESH
LOW = jnp.bfloat16
EDGES = (0, 2, 4, 7, 8)
CHUNKS = len(EDGES) - 1
WINDOW = 2
UNROLL = 13
WIDE = jnp.float32


def flipped(rank, step, count):
    total = 0
    bit = 1
    while bit < count:
        one = (rank // bit) % 2
        two = (step // bit) % 2
        total = total + bit * (one + two - 2 * one * two)
        bit *= 2
    return total


def contract(left, right, dims):
    return lax.dot_general(left, right, ((dims[:1], dims[1:]), ((), ())), preferred_element_type=WIDE)


def order(index, near, far, evens, subs):
    beside = max(near - 1, 1)
    second, third = index - subs, index - near * subs
    spot = third % max(far, 1)
    if evens:
        spot = 2 * (spot % evens) + spot // evens
    is_second = (second >= 0) * 1 - (third >= 0) * 1
    is_third = (third >= 0) * 1
    step = is_second * (1 + second % beside) + is_third * (near + spot)
    part = (1 - is_second - is_third) * index + is_second * (second // beside) + is_third * (third // max(far, 1))
    return step, part


def kernel(
    nq, nk, nka, subs,
    key_scale, value_scale, q_ref, g_ref, kc_ref, vc_ref,
    dq_hbm, dk_hbm, dv_hbm,
    dq_ref, dk_ref, dv_ref, leave, qd, kv, codes, held_e, held_d, shift, top, total, dot, stats, lse, delta, acc_q, acc_k, acc_v,
    gk_out, gk_mid, gk_in, gk_side, gq_out, gq_mid, gq_in,
    load, q_send, q_recv, k_send, k_recv, s_send, s_recv,
    gk_send, gk_mid_recv, gk_recv, gq_send, gq_mid_recv, gq_recv, side_send, side_recv,
):
    rows, width = q_ref.shape
    slab = rows // subs
    factor = 1.0 / math.sqrt(width)
    log2e = math.log2(math.e)
    pb, ka = lax.axis_index("pb"), lax.axis_index("ka")
    my_a, my_k = pb // nk, pb % nk
    my_q = my_a * nka + ka
    near_u, near_w, far_w, even_w = nka * subs, 2 * subs, nk - 2, nk // 2 - 1

    def q_rank(step):
        return flipped(my_q, step, nq)

    def q_peer(step):
        rank = q_rank(step)
        return {"pb": (rank // nka) * nk + my_k, "ka": rank % nka}

    def k_peer(step):
        return {"pb": my_a * nk + flipped(my_k, step, nk), "ka": ka}

    def chunk(part):
        unit = rows // EDGES[-1]
        return pl.ds(EDGES[part] * unit, (EDGES[part + 1] - EDGES[part]) * unit)

    def q_copy(source, to, part):
        span = chunk(part)
        return pltpu.make_async_remote_copy(
            qd.at[source, :, span], qd.at[source ^ to, :, span],
            q_send.at[source ^ to, part], q_recv.at[source ^ to, part],
            device_id=q_peer(to), device_id_type=MESH)

    def k_copy(source, to, part):
        span = chunk(part)
        return pltpu.make_async_remote_copy(
            kv.at[source, :, span], kv.at[source ^ to, :, span],
            k_send.at[source ^ to, part], k_recv.at[source ^ to, part],
            device_id=k_peer(to), device_id_type=MESH)

    def s_copy(to):
        return pltpu.make_async_remote_copy(
            stats.at[0], stats.at[to], s_send.at[to], s_recv.at[to],
            device_id=q_peer(to), device_id_type=MESH)

    def gk_copy(step, part):
        span = pl.ds(part * slab, slab)
        return pltpu.make_async_remote_copy(
            gk_out.at[step, :, span], gk_in.at[step, :, span], gk_send.at[step, part], gk_recv.at[step, part],
            device_id=k_peer(step), device_id_type=MESH)

    def gk_mid_copy(step, part):
        span = pl.ds(part * slab, slab)
        kinds = pl.ds(0, 1 if part == subs - 1 else 2)
        return pltpu.make_async_remote_copy(
            gk_out.at[step, kinds, span], gk_mid.at[step ^ 1, kinds, span],
            gk_send.at[step, part], gk_mid_recv.at[step ^ 1, part],
            device_id=k_peer(1), device_id_type=MESH)

    def gk_side_copy(step):
        span = pl.ds((subs - 1) * slab, slab)
        return pltpu.make_async_remote_copy(
            gk_out.at[step, 1, span], gk_side.at[step ^ 1], side_send.at[step], side_recv.at[step ^ 1],
            device_id=k_peer(step ^ 1), device_id_type=MESH)

    def gq_copy(step, part):
        span = pl.ds(part * slab, slab)
        return pltpu.make_async_remote_copy(
            gq_out.at[step, span], gq_in.at[step, span], gq_send.at[step, part], gq_recv.at[step, part],
            device_id=q_peer(step), device_id_type=MESH)

    def gq_mid_copy(step, part):
        span = pl.ds(part * slab, slab)
        return pltpu.make_async_remote_copy(
            gq_out.at[step, span], gq_mid.at[step - nka, span],
            gq_send.at[step, part], gq_mid_recv.at[step - nka, part],
            device_id=q_peer(step - nka), device_id_type=MESH)

    barrier = pltpu.get_barrier_semaphore()
    for step in range(1, nq):
        pl.semaphore_signal(barrier, inc=1, device_id=q_peer(step), device_id_type=MESH)
    for step in range(1, nk):
        pl.semaphore_signal(barrier, inc=1, device_id=k_peer(step), device_id_type=MESH)
    loads = [
        pltpu.make_async_copy(q_ref, qd.at[0, 0], load.at[0]),
        pltpu.make_async_copy(g_ref, qd.at[0, 1], load.at[1]),
        pltpu.make_async_copy(kc_ref, codes.at[0], load.at[2]),
        pltpu.make_async_copy(vc_ref, codes.at[1], load.at[3]),
    ]
    for one in loads:
        one.start()
    for one in loads:
        one.wait()
    kv[0, 0] = (codes[0].astype(WIDE) * key_scale[0]).astype(LOW)
    kv[0, 1] = (codes[1].astype(WIDE) * value_scale[0]).astype(LOW)
    pl.semaphore_wait(barrier, nq + nk - 2)

    def own_copies(part):
        return [
            *[k_copy(0, step, part) for step in range(2, nk, 2)],
            q_copy(0, nka, part),
            k_copy(0, 1, part),
            *[q_copy(0, step, part) for step in range(1, nka)],
        ]

    for part in range(WINDOW):
        for one in own_copies(part):
            one.start()
    top[...] = jnp.full_like(top, -1e30)
    total[...] = jnp.zeros_like(total)
    dot[...] = jnp.zeros_like(dot)
    acc_q[...] = jnp.zeros_like(acc_q)
    acc_k[...] = jnp.zeros_like(acc_k)
    acc_v[...] = jnp.zeros_like(acc_v)

    def serve(part):
        if part + WINDOW < CHUNKS:
            for one, other in zip(own_copies(part), own_copies(part + WINDOW)):
                one.wait_send()
                other.start()
        q_copy(0, nka, part).wait_recv()
        for step in range(1, nka):
            q_copy(nka, step, part).start()
        for step in range(2, nk, 2):
            k_copy(0, step, part).wait_recv()
            k_copy(step, 1, part).start()

    def q_place(u):
        return order(u, nka, nka, 0, subs)

    def k_place(w):
        return order(w, 2, far_w, even_w, subs)

    def first(u, w):
        (j, a), (i, b) = q_place(u), k_place(w)
        span_q, span_k = pl.ds(a * slab, slab), pl.ds(b * slab, slab)
        shape = (slab // 8, 8, slab)
        scores = (contract(kv[i, 0, span_k], qd[j, 0, span_q], (1, 1)) * (factor * log2e)).reshape(shape)
        d_probs = contract(kv[i, 1, span_k], qd[j, 1, span_q], (1, 1))
        old_top = top[u]
        new_top = jnp.maximum(old_top, jnp.max(scores, axis=0))
        shifted = jnp.exp2(scores - new_top[None])
        old = jnp.exp2(old_top - new_top)
        total[u] = total[u] * old + jnp.sum(shifted, axis=0)
        dot[u] = dot[u] * old + jnp.sum(shifted * d_probs.reshape(shape), axis=0)
        top[u] = new_top
        shift[u, i, b] = new_top
        held_e[u, i, span_k] = shifted.reshape(slab, slab)
        held_d[u, i, span_k] = d_probs

    def first_over(us, ws):
        count = len(us) * len(ws)
        if count == 0:
            return

        @pl.loop(0, count, unroll=max(n for n in range(1, UNROLL + 1) if count % n == 0))
        def _(n):
            first(us.start + n // len(ws), ws.start + n % len(ws))

    first_over(range(subs), range(subs))
    end_u, end_w, served, share = subs, subs, 0, CHUNKS // subs
    for group in range(subs):
        while served < max(1, (group + 1) * share - WINDOW):
            serve(served)
            served += 1
        for part in range(group * share, (group + 1) * share):
            for step in range(1, nka):
                q_copy(0, step, part).wait_recv()
            k_copy(0, 1, part).wait_recv()
        first_over(range(end_u), range(end_w, end_w + 1))
        first_over(range(end_u, end_u + nka - 1), range(end_w + 1))
        end_u, end_w = end_u + nka - 1, end_w + 1
    for group in range(subs):
        while served < (group + 1) * share:
            serve(served)
            served += 1
        first_over(range(end_u), range(end_w, end_w + even_w))
        first_over(range(end_u, end_u + 1), range(end_w + even_w))
        if served < CHUNKS:
            serve(served)
            served += 1
        for part in range(group * share, (group + 1) * share):
            for step in range(1, nka):
                q_copy(0, nka + step, part).wait_recv()
        first_over(range(end_u + 1, end_u + nka), range(end_w + even_w))
        for part in range(group * share, (group + 1) * share):
            for step in range(3, nk, 2):
                k_copy(0, step, part).wait_recv()
        first_over(range(end_u + nka), range(end_w + even_w, end_w + far_w))
        end_u, end_w = end_u + nka, end_w + far_w

    count_u = nq * subs
    for u in range(count_u):
        j, a = q_place(u)
        row = q_rank(j) * subs + a
        best = jnp.max(top[u], axis=0, keepdims=True)
        scale = jnp.exp2(top[u] - best)
        whole = jnp.sum(total[u] * scale, axis=0, keepdims=True)
        stats[0, pl.ds(row, 1), :] = best + jnp.log2(whole)
        stats[0, pl.ds(count_u + row, 1), :] = jnp.sum(dot[u] * scale, axis=0, keepdims=True) / whole
    for step in range(nq - 1, 0, -1):
        s_copy(step).start()
    for step in range(1, nq):
        s_copy(step).wait_recv()
    parts = [stats[r, 0:count_u, :] for r in range(nq)]
    best = functools.reduce(jnp.maximum, parts)
    weights = [jnp.exp2(part - best) for part in parts]
    whole = sum(weights)
    lse[...] = best + jnp.log2(whole)
    delta[...] = sum(w * stats[r, count_u : 2 * count_u, :] for r, w in enumerate(weights)) / whole

    def second(u, p):
        j, a = q_place(u)
        i, b = turn(p)
        span, span_k = pl.ds(a * slab, slab), pl.ds(b * slab, slab)
        row = pl.ds(q_rank(j) * subs + a, 1)
        shape = (slab // 8, 8, slab)
        queries, grads = qd[j, 0, span], qd[j, 1, span]
        scale = jnp.exp2(shift[u, i, b] - lse[row, :])
        probs = held_e[u, i, span_k].reshape(shape) * scale[None]
        d_scores = probs * (held_d[u, i, span_k].reshape(shape) - delta[row, :][None])
        d_scores = d_scores.reshape(slab, slab).astype(LOW)
        acc_v[i, span_k] += contract(probs.reshape(slab, slab).astype(LOW), grads, (1, 0))
        acc_k[i, span_k] += contract(d_scores, queries, (1, 0))
        acc_q[u] += contract(kv[i, 0, span_k], d_scores, (0, 0))

    def turn(p):
        nth = p // subs
        odd, early = (nth < even_w) * 1, (nth < 2 * even_w) * 1
        even = (early - odd) * 2 * (nth - even_w + 1) + (1 - early) * (nk - 1 - nth)
        return odd * (nk - 1 - 2 * nth) + even, p % subs

    def second_over(us, ps):
        count = len(us) * len(ps)
        if count == 0:
            return

        @pl.loop(0, count, unroll=max(n for n in range(1, UNROLL + 1) if count % n == 0))
        def _(n):
            second(us.start + n // len(ps), ps.start + n % len(ps))

    def pack_keys(i, b):
        span = pl.ds(b * slab, slab)
        gk_out[i, 0, span] = (acc_k[i, span] * factor).astype(LOW)
        gk_out[i, 1, span] = acc_v[i, span].astype(LOW)

    def query_part(u):
        return acc_q[u].T * factor

    def send_queries(u):
        j, a = q_place(u)
        gq_out[j, pl.ds(a * slab, slab)] = query_part(u).astype(LOW)
        (gq_mid_copy if j > nka else gq_copy)(j, a).start()

    def send_far(u):
        _, a = q_place(u)
        span = pl.ds(a * slab, slab)
        far = query_part(u)
        for step in range(1, nka):
            gq_mid_copy(nka + step, a).wait_recv()
            far = far + gq_mid[step, span].astype(WIDE)
        gq_out[nka, span] = far.astype(LOW)
        gq_copy(nka, a).start()

    last, mids = nk * subs, even_w * subs
    beside = last - 2 * subs
    for p in range(mids):
        second_over(range(count_u), range(p, p + 1))
        i, b = turn(p)
        pack_keys(i, b)
        gk_mid_copy(i, b).start()
        if b == subs - 1:
            gk_side_copy(i).start()
    for group in range(subs):
        begin = near_u + group * nka
        second_over(range(begin + 1, begin + nka), range(mids, last))
        for u in range(begin + 1, begin + nka):
            send_queries(u)

    def send_even(b):
        span = pl.ds(b * slab, slab)
        for i in range(2, nk, 2):
            gk_mid_copy(i ^ 1, b).wait_recv()
            gk_out[i, 0, span] = (acc_k[i, span] * factor + gk_mid[i, 0, span].astype(WIDE)).astype(LOW)
            value_sum = acc_v[i, span]
            if b < subs - 1:
                value_sum = value_sum + gk_mid[i, 1, span].astype(WIDE)
            gk_out[i, 1, span] = value_sum.astype(LOW)
            gk_copy(i, b).start()

    second_over(range(near_u), range(mids, beside))
    for group in range(subs):
        second_over(range(near_u + group * nka, near_u + group * nka + 1), range(mids, last))
    for b in range(subs - 1):
        send_even(b)
        send_far(near_u + b * nka)
    second_over(range(near_u), range(beside, beside + subs))
    send_even(subs - 1)
    send_far(near_u + (subs - 1) * nka)
    for b in range(subs):
        pack_keys(1, b)
        if b == subs - 1 and nk > 2:
            span = pl.ds(b * slab, slab)
            value_sum = acc_v[1, span]
            for i in range(2, nk, 2):
                gk_side_copy(i ^ 1).wait_recv()
                value_sum = value_sum + gk_side[i].astype(WIDE)
            gk_out[1, 1, span] = value_sum.astype(LOW)
        gk_copy(1, b).start()
    second_over(range(subs, near_u), range(last - subs, last))
    for u in range(subs, near_u):
        send_queries(u)
    second_over(range(subs), range(last - subs, last))

    def out_copy(n, part):
        span = pl.ds(part * slab, slab)
        source, target = ((dq_ref, dq_hbm), (dk_ref, dk_hbm), (dv_ref, dv_hbm))[n]
        return pltpu.make_async_copy(source.at[span], target.at[span], leave.at[n, part])

    for a in range(subs):
        span = pl.ds(a * slab, slab)
        query_total = query_part(a)
        for step in range(1, nka + 1):
            gq_copy(step, a).wait_recv()
            query_total = query_total + gq_in[step, span].astype(WIDE)
        dq_ref[span, :] = query_total
        out_copy(0, a).start()
    for b in range(subs):
        span = pl.ds(b * slab, slab)
        key_sum, value_sum = acc_k[0, span] * factor, acc_v[0, span]
        for step in (*range(2, nk, 2), 1):
            gk_copy(step, b).wait_recv()
            key_sum = key_sum + gk_in[step, 0, span].astype(WIDE)
            value_sum = value_sum + gk_in[step, 1, span].astype(WIDE)
        dk_ref[span, :] = key_sum
        dv_ref[span, :] = value_sum
        out_copy(1, b).start()
        out_copy(2, b).start()
    for part in range(CHUNKS):
        if part + WINDOW >= CHUNKS:
            for one in own_copies(part):
                one.wait_send()
        for step in range(1, nka):
            q_copy(nka, step, part).wait_send()
        for step in range(2, nk, 2):
            k_copy(step, 1, part).wait_send()
    for step in range(1, nq):
        s_copy(step).wait_send()
        for part in range(subs):
            gq_copy(step, part).wait_send()
    for step in range(1, nk):
        relayed = step > 1 and step % 2 == 1
        for part in range(subs):
            (gk_mid_copy if relayed else gk_copy)(step, part).wait_send()
        if relayed:
            gk_side_copy(step).wait_send()
    for n in range(3):
        for part in range(subs):
            out_copy(n, part).wait()


def tail(dq_in, dk_in, dv_in, dq_ref, dk_ref, dv_ref):
    dq_ref[...] = dq_in[...]
    dk_ref[...] = dk_in[...]
    dv_ref[...] = dv_in[...]


def shards(queries, key_codes, value_codes, key_scale, value_scale, out_grad):
    rows, width = queries.shape
    npb, nka = lax.axis_size("pb"), lax.axis_size("ka")
    nq, nk = 2 * nka, npb // 2
    subs = max(rows // 256, 1)
    slab = rows // subs
    vmem = pl.BlockSpec(memory_space=pltpu.VMEM)
    hbm = pl.BlockSpec(memory_space=pltpu.HBM)
    smem = pl.BlockSpec(memory_space=pltpu.SMEM)
    out = jax.ShapeDtypeStruct((rows, width), WIDE)
    counts = (
        (4,), *[(n, CHUNKS) for n in (nq, nq, nk, nk)],
        (nq,), (nq,), *[(n, subs) for n in (nk, nk, nk, nq, nka, nq)], (nk,), (nk,),
    )
    sems = [pltpu.SemaphoreType.DMA(count) for count in counts]
    places = nq * subs
    grads = pl.pallas_call(
        functools.partial(kernel, nq, nk, nka, subs),
        out_shape=(out, out, out),
        in_specs=[smem, smem, hbm, hbm, hbm, hbm],
        out_specs=(hbm, hbm, hbm),
        scratch_shapes=[
            *[pltpu.VMEM((rows, width), WIDE)] * 3,
            pltpu.SemaphoreType.DMA((3, subs)),
            pltpu.VMEM((nq, 2, rows, width), LOW),
            pltpu.VMEM((nk, 2, rows, width), LOW),
            pltpu.VMEM((2, rows, width), jnp.int32),
            pltpu.VMEM((places, nk, rows, slab), WIDE),
            pltpu.VMEM((places, nk, rows, slab), WIDE),
            pltpu.VMEM((places, nk, subs, 8, slab), WIDE),
            pltpu.VMEM((places, 8, slab), WIDE),
            pltpu.VMEM((places, 8, slab), WIDE),
            pltpu.VMEM((places, 8, slab), WIDE),
            pltpu.VMEM((nq, 2 * places, slab), WIDE),
            pltpu.VMEM((places, slab), WIDE),
            pltpu.VMEM((places, slab), WIDE),
            pltpu.VMEM((places, width, slab), WIDE),
            pltpu.VMEM((nk, rows, width), WIDE),
            pltpu.VMEM((nk, rows, width), WIDE),
            *[pltpu.VMEM((nk, 2, rows, width), LOW)] * 3,
            pltpu.VMEM((nk, slab, width), LOW),
            pltpu.VMEM((nq, rows, width), LOW),
            pltpu.VMEM((nka, rows, width), LOW),
            pltpu.VMEM((nq, rows, width), LOW),
            *sems,
        ],
        compiler_params=pltpu.CompilerParams(
            collective_id=0, has_side_effects=True, vmem_limit_bytes=60 << 20
        ),
    )(key_scale.reshape(1), value_scale.reshape(1), queries, out_grad, key_codes, value_codes)
    return tuple(pl.pallas_call(tail, out_shape=(out, out, out), in_specs=[vmem] * 3, out_specs=(vmem,) * 3)(*grads))


def solution(mesh):
    in_specs = (
        P(("pb", "ka"), "ha"),
        P(("ka", "pb"), "ha"),
        P(("ka", "pb"), "ha"),
        P(),
        P(),
        P(("pb", "ka"), "ha"),
    )
    out_specs = (P(("pb", "ka"), "ha"), P(("ka", "pb"), "ha"), P(("ka", "pb"), "ha"))
    return jax.shard_map(shards, mesh=mesh, in_specs=in_specs, out_specs=out_specs, check_vma=False)
```
